32 devices in a mesh: row: 8 (over y, x, core), col: 4 (over z).
Axes of the slice: x: 2, y: 2, z: 4, core: 2. Of those that a mesh axis runs over, the one named last changes fastest.
Arguments:
- sparse_tiles: bfloat16 [128, 7, 128, 128], P(('row', 'col')), may hold values from -0.125 to 0.125
- tile_columns: int32 [128, 7], P(('row', 'col')), may hold values from 0 to 7, as said below
- block_counts: int32 [128], P(('row', 'col')), may hold values from 1 to 7, as said below
- krylov_first: bfloat16 [4096, 256], P(('row', 'col')), may hold values from -6 to 6
- panel_block: bfloat16 [4096, 256], P(('row', 'col')), may hold values from -1 to 1
Outputs:
- triangle_factor: float32 [256, 256], replicated
- coefficients: float32 [256, 768], replicated
- projected: bfloat16 [4096, 768], P(('row', 'col'))
The draws below stay inside these ranges and needn't reach their ends.
Inputs may be any that keep to these rules, and one draw needn't show every extreme that they name: `tile_columns`: distinct along the last dimension. `block_counts`: some aligned block of 4 entries holds 7 in every entry.
All inputs are finite; a program needn't handle non-finite values.
Results may differ from the reference program's by a relative error of at most 0.0049.
Values may be sent and summed in bfloat16 or wider, within the bound.
A program may use at most 64 MiB of HBM per device.

```python
import math
import jax
import jax.numpy as jnp
from jax import lax

PANEL = 256
TILE = 128
DEG_MAX = 7
ROWS_DEV = 128
NODES = 4096
RB_LOC = 4
CB_LOC = 8
N_ROW = 8
N_COL = 4


def draw_panel_block(key, part):
    first, second = jax.random.split(jax.random.fold_in(key, 11), 2)
    normal_part = jax.random.normal(first, (NODES, PANEL), jnp.float32)
    mixing = jnp.eye(PANEL, dtype=jnp.float32) + 0.6 * PANEL ** (-0.5) * jax.random.normal(second, (PANEL, PANEL), jnp.float32)
    values = jnp.dot(normal_part, mixing)
    rising = 1.0 + 2.0 * jnp.arange(NODES, dtype=jnp.float32) / NODES
    values = values * rising[:, None]
    values = values / math.sqrt(NODES)
    return jnp.clip(values, -1.0, 1.0).astype(jnp.bfloat16)


def draw_tile_columns(key, part):
    slot_rows = NODES * N_COL // TILE
    subkeys = jax.random.split(jax.random.fold_in(key, 21), slot_rows)

    def pick_order(subkey):
        return jax.random.permutation(subkey, CB_LOC)
    orders = jax.vmap(pick_order)(subkeys)
    return orders[:, :DEG_MAX].astype(jnp.int32)


def draw_block_counts(key, part):
    first, second, third = jax.random.split(jax.random.fold_in(key, 31), 3)
    base = jax.random.randint(first, (N_ROW, N_COL, RB_LOC), 1, 4)
    heavy = jax.random.randint(second, (N_ROW, 1, RB_LOC), 0, 4)
    factor = jnp.where(heavy == 3, 3, 1)
    counts = jnp.minimum(base * factor, DEG_MAX)
    fullest = jax.random.randint(third, (), 0, N_ROW * N_COL)
    flat = counts.reshape(N_ROW * N_COL, RB_LOC)
    marked = jnp.arange(N_ROW * N_COL) == fullest
    flat = jnp.where(marked[:, None], DEG_MAX, flat)
    return flat.reshape(-1).astype(jnp.int32)


def levels(stream_key, dims, cuts, least, top_value):
    level, own = 1.0, jax.random.fold_in(stream_key, 6)
    for dim, shards_of in cuts:
        draws = jnp.exp(jax.random.uniform(jax.random.fold_in(own, dim), (shards_of,), jnp.float32, least / len(cuts), top_value / len(cuts)))
        level = level * jnp.repeat(draws, dims[dim] // shards_of).reshape([-1 if axis == dim else 1 for axis in range(len(dims))])
    return level


def scatter_about(own_key, extent, spread, most, pieces=(), kind=jnp.bfloat16):
    gain = levels(own_key, extent, pieces, -0.22, 0.18) if pieces else 1.0
    drawn = jax.random.normal(own_key, extent, jnp.float32) * spread * gain
    return jnp.minimum(jnp.maximum(drawn, -most), most).astype(kind)


def setup_inputs(seed: int = 0) -> dict:
    key_list = jax.random.split(jax.random.key(seed), 6)
    return {
        "sparse_tiles": scatter_about(key_list[0], (NODES * N_COL // TILE, DEG_MAX, TILE, TILE), (TILE * DEG_MAX * N_COL // 2) ** -0.5, 0.125, ((0, 32),)),
        "tile_columns": draw_tile_columns(jax.random.fold_in(key_list[5], 71), 0),
        "block_counts": draw_block_counts(jax.random.fold_in(key_list[5], 71), 0),
        "krylov_first": scatter_about(key_list[3], (NODES, PANEL), 1.0, 6.0, ((0, 32),)),
        "panel_block": draw_panel_block(jax.random.fold_in(key_list[5], 71), 0),
    }


def factor_small(block):
    order = block.shape[0]
    positions = lax.broadcasted_iota(jnp.int32, (order,), 0)

    def one_column(index, state):
        working, lower, inverse = state
        column = lax.dynamic_slice_in_dim(working, index, 1, 1)[:, 0]
        pivot = jnp.sqrt(lax.dynamic_slice_in_dim(column, index, 1, 0)[0])
        column = jnp.where(positions >= index, column / pivot, jnp.zeros((), column.dtype))
        lower = lax.dynamic_update_slice_in_dim(lower, column[:, None], index, 1)
        working = working - column[:, None] * column[None, :]
        new_row = lax.dynamic_slice_in_dim(inverse, index, 1, 0) / pivot
        below = jnp.where(positions > index, column, jnp.zeros((), column.dtype))
        inverse = inverse - below[:, None] * new_row
        inverse = lax.dynamic_update_slice_in_dim(inverse, new_row, index, 0)
        return (working, lower, inverse)
    start = (block, jnp.zeros_like(block), jnp.eye(order, dtype=block.dtype))
    _, lower, inverse = lax.fori_loop(0, order, one_column, start)
    return (lower, inverse)

def factor_panel(gram_matrix):
    order = gram_matrix.shape[0]
    width = order // 4
    working = gram_matrix
    column_blocks = []
    diag_inverses = []
    for block_index in range(4):
        low = block_index * width
        lower_diag, inverse_diag = factor_small(working[:width, :width])
        under = jnp.dot(working[width:, :width], inverse_diag.T, precision=lax.Precision.HIGHEST)
        working = working[width:, width:] - jnp.dot(under, under.T, precision=lax.Precision.HIGHEST)
        column_blocks.append(jnp.concatenate([jnp.zeros((low, width), gram_matrix.dtype), lower_diag, under], axis=0))
        diag_inverses.append(inverse_diag)
    lower = jnp.concatenate(column_blocks, axis=1)
    identity = jnp.eye(order, dtype=gram_matrix.dtype)
    inverse_rows = []
    for block_index in range(4):
        low = block_index * width
        high = low + width
        target = identity[low:high, :]
        if block_index > 0:
            earlier = jnp.concatenate(inverse_rows, axis=0)
            target = target - jnp.dot(lower[low:high, :low], earlier, precision=lax.Precision.HIGHEST)
        inverse_rows.append(jnp.dot(diag_inverses[block_index], target, precision=lax.Precision.HIGHEST))
    return (lower, jnp.concatenate(inverse_rows, axis=0))

def multiply(source, sparse_tiles, tile_columns, block_counts):
    columns = source.shape[1]
    blocks = source.reshape(N_ROW, N_COL, ROWS_DEV, columns)
    by_column = jnp.transpose(blocks, (1, 0, 2, 3)).reshape(N_COL, CB_LOC, TILE, columns)
    tile_grid = sparse_tiles.reshape(N_ROW, N_COL, RB_LOC, DEG_MAX, TILE, TILE)
    column_grid = tile_columns.reshape(N_ROW, N_COL, RB_LOC, DEG_MAX)
    count_grid = block_counts.reshape(N_ROW, N_COL, RB_LOC)
    slot_index = lax.broadcasted_iota(jnp.int32, (RB_LOC, DEG_MAX), 1)

    def one_row(row_index):

        def one_column(running, col_index):
            picked = jnp.take(by_column[col_index], column_grid[row_index, col_index], axis=0)
            active = slot_index < count_grid[row_index, col_index][:, None]
            picked = jnp.where(active[:, :, None, None], picked.astype(jnp.float32), jnp.zeros((), jnp.float32))
            tile_term = jnp.einsum('bkij,bkjw->biw', tile_grid[row_index, col_index].astype(jnp.float32), picked)
            return (running + tile_term, None)
        start = jnp.zeros((RB_LOC, TILE, columns), jnp.float32)
        summed, _ = lax.scan(one_column, start, jnp.arange(N_COL, dtype=jnp.int32))
        return summed.reshape(RB_LOC * TILE, columns)
    rows_all = lax.map(one_row, jnp.arange(N_ROW, dtype=jnp.int32))
    return rows_all.reshape(NODES, columns).astype(jnp.bfloat16)

def reference(sparse_tiles, tile_columns, block_counts, krylov_first, panel_block):
    krylov_second = multiply(krylov_first, sparse_tiles, tile_columns, block_counts)
    krylov_third = multiply(krylov_second, sparse_tiles, tile_columns, block_counts)
    trailing = jnp.concatenate([krylov_first, krylov_second, krylov_third], axis=1)
    gram_matrix = jnp.dot(panel_block.T, panel_block, preferred_element_type=jnp.float32)
    cross_terms = jnp.dot(panel_block.T, trailing, preferred_element_type=jnp.float32)
    lower_factor, lower_inverse = factor_panel(gram_matrix)
    coefficients = jnp.dot(lower_inverse, cross_terms, precision=lax.Precision.HIGHEST)
    weights = jnp.dot(lower_inverse.T, coefficients, precision=lax.Precision.HIGHEST)
    removed = jnp.dot(panel_block.astype(jnp.float32), weights, precision=lax.Precision.HIGHEST)
    projected = (trailing.astype(jnp.float32) - removed).astype(jnp.bfloat16)
    return (lower_factor.T, coefficients, projected)
```

```python
import functools

import jax
import jax.numpy as jnp
from jax import lax
from jax.experimental import pallas as pl
from jax.experimental.pallas import tpu as pltpu
from jax.sharding import PartitionSpec as P

HIGHEST = lax.Precision.HIGHEST
F32 = jnp.float32
BF16 = jnp.bfloat16


def dot_nn(a, b, precision=None):
    return lax.dot_general(a, b, (((1,), (0,)), ((), ())), precision=precision, preferred_element_type=F32)


def dot_nt(a, b, precision=None):
    return lax.dot_general(a, b, (((1,), (1,)), ((), ())), precision=precision, preferred_element_type=F32)


def dot_tn(a, b, precision=None):
    return lax.dot_general(a, b, (((0,), (0,)), ((), ())), precision=precision, preferred_element_type=F32)


def eliminate(diag):
    width = diag.shape[0]
    wide = (8, 2 * width)
    low = lax.broadcasted_iota(jnp.int32, (width, width), 0)
    high = lax.broadcasted_iota(jnp.int32, (width, width), 1)
    sub = lax.broadcasted_iota(jnp.int32, wide, 0)
    work = jnp.concatenate([diag, (low == high).astype(F32)], axis=1)
    head = [jnp.broadcast_to(work[:8, k : k + 1], wide) for k in range(8)]
    done = []
    for at in range(0, width, 8):
        rest = width - at - 8
        rows, below = work[:8], work[8:]
        if rest:
            tail = [jnp.broadcast_to(below[:, at + k : at + k + 1], (rest, 2 * width)) for k in range(8)]
            ahead = [jnp.broadcast_to(below[:8, at + k + 8 : at + k + 9], wide) for k in range(8)]
        scale = jnp.zeros(wide, F32)
        for i in range(8):
            inverse = 1.0 / jnp.broadcast_to(head[i][i : i + 1], wide)
            factor = jnp.where(sub > i, head[i] * inverse, 0.0)
            scale = jnp.where(sub == i, inverse, scale)
            if rest:
                under = tail[i] * inverse[:1]
                for k in range(8):
                    ahead[k] = ahead[k] - under[:8] * tail[i][k : k + 1]
                for k in range(i + 1, 8):
                    tail[k] = tail[k] - under * head[k][i : i + 1]
                below = below - under * rows[i : i + 1]
            for k in range(i + 1, 8):
                head[k] = head[k] - factor * head[k][i : i + 1]
            rows = rows - factor * rows[i : i + 1]
        done.append(rows * jnp.sqrt(scale))
        if rest:
            head, work = ahead, below
    both = jnp.concatenate(done, axis=0)
    upper = jnp.where(high >= low, both[:, :width], 0.0)
    inverse = jnp.where(high <= low, both[:, width:], 0.0)
    return upper, inverse


def over_chunks(total, chunk, run):
    if total <= chunk:
        run(0, total)
    else:
        def one(index, carry):
            run(pl.multiple_of(index * chunk, chunk), chunk)
            return carry

        lax.fori_loop(0, total // chunk, one, 0)


def body(n_row, n_col, degree, row_blocks, tile,
         tiles_hbm, columns_ref, counts_ref, first_ref, panel_ref,
         lower_ref, upper_out, cross_out, second_ref, third_ref,
         tiles_ref, dense_ref, gathered_a, gathered_b, panels_ref, sums_ref, send_a, send_b, get_a, get_b,
         parts, cores, halves, takes, mixes, fulls, turned_ref,
         tile_sem, gs_sem, gr_sem, gfs_sem, gfr_sem, ps_sem, pr_sem, ss_sem, sr_sem,
         cs_sem, cr_sem, rs_sem, rr_sem, xs_sem, xr_sem, as_sem, ar_sem, afs_sem, afr_sem):
    row = lax.axis_index("row")
    col = lax.axis_index("col")
    panel_width = panel_ref.shape[1]
    rows_dev = panel_ref.shape[0]
    n_chip = n_row // 2
    chip = row // 2
    core = lax.rem(row, 2)
    other = 1 - core
    partner = chip * 2 + other
    mesh_type = pl.DeviceIdType.MESH

    load_tiles = pltpu.make_async_copy(tiles_hbm, tiles_ref, tile_sem)
    load_tiles.start()

    def ahead(step):
        return lax.rem(chip + step, n_chip)

    def behind(step):
        return lax.rem(chip + n_chip - step, n_chip)

    def col_peer(step):
        return lax.rem(col + step, n_col)

    barrier = pltpu.get_barrier_semaphore()
    pl.semaphore_signal(barrier, inc=1, device_id=(partner, col), device_id_type=mesh_type)
    for step in range(1, n_chip):
        pl.semaphore_signal(barrier, inc=1, device_id=(ahead(step) * 2 + core, col), device_id_type=mesh_type)
    for step in range(1, n_col):
        pl.semaphore_signal(barrier, inc=1, device_id=(row, col_peer(step)), device_id_type=mesh_type)

    everything = []

    def begin(copies):
        for copy in copies:
            copy.start()
        everything.extend(copies)
        return copies

    def arrive(copies):
        for copy in copies:
            copy.wait_recv()

    def to_partner(source, target, send_sem, recv_sem):
        return pltpu.make_async_remote_copy(
            src_ref=source, dst_ref=target, send_sem=send_sem, recv_sem=recv_sem,
            device_id=(partner, col), device_id_type=mesh_type)

    def over_chips(source, target, send_sem, recv_sem):
        return [
            pltpu.make_async_remote_copy(
                src_ref=source(step), dst_ref=target(step),
                send_sem=send_sem.at[step], recv_sem=recv_sem.at[step],
                device_id=(ahead(step) * 2 + core, col), device_id_type=mesh_type)
            for step in range(1, n_chip)
        ]

    def over_col(source, target, send_sem, recv_sem):
        return [
            pltpu.make_async_remote_copy(
                src_ref=source(step), dst_ref=target(step),
                send_sem=send_sem.at[step], recv_sem=recv_sem.at[step],
                device_id=(row, col_peer(step)), device_id_type=mesh_type)
            for step in range(1, n_col)
        ]

    def gather(source, slots, sems):
        send, recv, pass_send, pass_recv = sems
        copies = begin(over_chips(lambda s: source, lambda s: slots(core, chip), send, recv))
        near = begin([to_partner(source, slots(core, chip), pass_send.at[0], pass_recv.at[0])])
        return copies, near

    def relay(state, slots, sems):
        copies, near = state
        send, recv, pass_send, pass_recv = sems
        passed = list(near)
        for step, copy in enumerate(copies, start=1):
            copy.wait_recv()
            here = slots(core, behind(step))
            passed += begin([to_partner(here, here, pass_send.at[step], pass_recv.at[step])])
        return passed

    def gather_sems(index):
        return gs_sem.at[index], gr_sem.at[index], gfs_sem.at[index], gfr_sem.at[index]

    def share_sems(index):
        return as_sem.at[index], ar_sem.at[index], afs_sem.at[index], afr_sem.at[index]

    def fold(part_ref, core_ref, index):
        return begin([to_partner(part_ref.at[other], core_ref, cs_sem.at[index], cr_sem.at[index])])

    def spread(folded, part_ref, core_ref, half_ref, take_ref, index):
        arrive(folded)
        half_ref[...] = (part_ref[core].astype(F32) + core_ref[...].astype(F32)).astype(half_ref.dtype)
        return begin(over_chips(lambda s: half_ref.at[ahead(s)], lambda s: take_ref.at[s],
                                rs_sem.at[index], rr_sem.at[index]))

    def strip_sum(copies, half_ref, take_ref):
        total = half_ref[chip].astype(F32)
        arrive(copies)
        for step in range(1, n_chip):
            total = total + take_ref[step].astype(F32)
        return total

    def put(value, part_ref, at):
        width = value.shape[1]
        part_ref[:, :, :, at : at + width] = value.reshape(part_ref.shape[:3] + (width,))

    def exchange(total, mix_ref, index):
        mix_ref[col] = total
        return begin(over_col(lambda s: mix_ref.at[col], lambda s: mix_ref.at[col],
                              xs_sem.at[index], xr_sem.at[index]))

    def share(copies, mix_ref, full_ref, index):
        arrive(copies)
        total = mix_ref[0]
        for c in range(1, n_col):
            total = total + mix_ref[c]
        full_ref[core, chip] = total
        return gather(full_ref.at[core, chip], lambda k, q: full_ref.at[k, q], share_sems(index))

    def whole(full_ref):
        return full_ref[...].reshape(panel_width, full_ref.shape[3])

    def product(gathered_ref, send_ref):
        right = gathered_ref[...].reshape(n_row * rows_dev, panel_width)

        def run(at, size):
            sums_ref[pl.ds(at, size), :] = dot_nn(dense_ref[pl.ds(at, size), :], right)

        over_chunks(row_blocks * tile, 4 * tile, run)
        for c in range(n_col):
            send_ref[c] = sums_ref[c * rows_dev : (c + 1) * rows_dev, :].astype(BF16)

    def scatter(send_ref, get_ref, index):
        return begin(over_col(lambda s: send_ref.at[col_peer(s)], lambda s: get_ref.at[s],
                              ss_sem.at[index], sr_sem.at[index]))

    def collect(copies, get_ref, result_ref):
        own = sums_ref[pl.ds(pl.multiple_of(col * rows_dev, 8), rows_dev), :]
        arrive(copies)
        for step in range(1, n_col):
            own = own + get_ref[step].astype(F32)
        result_ref[...] = own.astype(BF16)

    def slots_a(k, q):
        return gathered_a.at[q * 2 + k]

    def slots_b(k, q):
        return gathered_b.at[q * 2 + k]

    def stage(index, value):
        put(value, parts.at[index], 0)
        return fold(parts.at[index], cores.at[index], index)

    def spread_stage(index, folded):
        return spread(folded, parts.at[index], cores.at[index], halves.at[index], takes.at[index], index)

    def exchange_stage(index, copies):
        return exchange(strip_sum(copies, halves.at[index], takes.at[index]), mixes.at[index], index)

    def full_slots(index):
        return lambda k, q: fulls.at[index, k, q]

    def share_stage(index, copies):
        return share(copies, mixes.at[index], fulls.at[index], index)

    def relay_stage(index, state):
        return relay(state, full_slots(index), share_sems(index))

    panel = panel_ref[...]
    put(dot_tn(panel, panel), parts.at[0], 0)
    pl.semaphore_wait(barrier, n_chip + n_col - 1)

    gather_1 = gather(first_ref, slots_a, gather_sems(0))
    fold_0 = fold(parts.at[0], cores.at[0], 0)
    panels = begin(over_col(lambda s: panel_ref, lambda s: panels_ref.at[col], ps_sem, pr_sem))
    gathered_a[row] = first_ref[...]
    panels_ref[col] = panel_ref[...]

    load_tiles.wait()
    column_blocks = n_row * rows_dev // tile

    def place(b):
        for j in range(column_blocks):
            slot = jnp.int32(0)
            live = jnp.int32(0)
            for k in range(degree):
                hit = jnp.logical_and(columns_ref[b, k] == j, k < counts_ref[0, b])
                slot = jnp.where(hit, k, slot)
                live = jnp.where(hit, 1, live)
            value = tiles_ref[b, slot]
            dense_ref[pl.ds(b * tile, tile), j * tile : (j + 1) * tile] = jnp.where(
                live > 0, value, jnp.zeros_like(value))

    if row_blocks <= 4:
        for b in range(row_blocks):
            place(b)
    else:
        def place_one(b, carry):
            place(b)
            return carry

        lax.fori_loop(0, row_blocks, place_one, 0)

    spread_0 = spread_stage(0, fold_0)
    passed_1 = relay(gather_1, slots_a, gather_sems(0))
    fold_1 = stage(1, dot_tn(panel, first_ref[...]))
    arrive(passed_1)
    product(gathered_a, send_a)
    scatter_1 = scatter(send_a, get_a, 0)
    exchange_0 = exchange_stage(0, spread_0)
    spread_1 = spread_stage(1, fold_1)
    collect(scatter_1, get_a, second_ref)
    gather_2 = gather(second_ref, slots_b, gather_sems(1))
    fold_2 = stage(2, dot_tn(panel, second_ref[...]))
    gathered_b[row] = second_ref[...]
    exchange_1 = exchange_stage(1, spread_1)
    share_0 = share_stage(0, exchange_0)
    spread_2 = spread_stage(2, fold_2)
    arrive(panels)
    turned_ref[...] = panels_ref[...].reshape(n_col * rows_dev, panel_width).T
    passed_2 = relay(gather_2, slots_b, gather_sems(1))
    exchange_2 = exchange_stage(2, spread_2)
    passed_s0 = relay_stage(0, share_0)
    arrive(passed_2)
    product(gathered_b, send_b)
    fold_3 = stage(3, dot_nn(turned_ref[...], send_b[...].reshape(n_col * rows_dev, panel_width)))
    scatter_2 = scatter(send_b, get_b, 1)
    spread_3 = spread_stage(3, fold_3)
    share_1 = share_stage(1, exchange_1)
    arrive(passed_s0)

    gram = whole(fulls.at[0])
    pieces = 4
    width = panel_width // pieces
    columns = [gram[width * j :, width * j : width * (j + 1)] for j in range(pieces)]
    uppers, inverses, unders = [], [], []

    def factor(b):
        upper, inverse = eliminate(columns[b][:width])
        under = None
        if b < pieces - 1:
            under = dot_nt(columns[b][width:], inverse, HIGHEST)
            for j in range(b + 1, pieces):
                o = (j - b - 1) * width
                columns[j] = columns[j] - dot_nt(under[o:], under[o : o + width], HIGHEST)
        uppers.append(upper)
        inverses.append(inverse)
        unders.append(under)

    factor(0)
    exchange_3 = exchange_stage(3, spread_3)
    passed_s1 = relay_stage(1, share_1)
    share_2 = share_stage(2, exchange_2)
    factor(1)
    share_3 = share_stage(3, exchange_3)
    passed_s2 = relay_stage(2, share_2)
    factor(2)
    passed_s3 = relay_stage(3, share_3)
    factor(3)

    identity = (lax.broadcasted_iota(jnp.int32, (width, panel_width), 1)
                - lax.broadcasted_iota(jnp.int32, (width, panel_width), 0))
    for b in range(pieces):
        target = (identity == b * width).astype(F32)
        for e in range(b):
            o = (b - e - 1) * width
            target = target - dot_nn(unders[e][o : o + width], lower_ref[e * width : (e + 1) * width, :], HIGHEST)
        lower_ref[b * width : (b + 1) * width, :] = dot_nn(inverses[b], target, HIGHEST)
    for b in range(pieces):
        parts = [jnp.zeros((width, b * width), F32)] if b else []
        parts.append(uppers[b])
        if b < pieces - 1:
            parts.append(unders[b].T)
        upper_out[b * width : (b + 1) * width, :] = jnp.concatenate(parts, axis=1)

    collect(scatter_2, get_b, third_ref)
    for index, passed in enumerate((passed_s1, passed_s2, passed_s3)):
        arrive(passed)
        cross_out[:, index * panel_width : (index + 1) * panel_width] = whole(fulls.at[index + 1])
    for copy in everything:
        copy.wait_send()


def project(lower_ref, upper_ref, cross_ref, first_ref, second_ref, third_ref, panel_ref,
            upper_out, coef_out, proj_out):
    block = pl.program_id(0)

    @pl.when(block == 0)
    def _():
        upper_out[...] = upper_ref[...]

    lower_inverse = lower_ref[...]
    coefficients = dot_nn(lower_inverse, cross_ref[...], HIGHEST)
    coef_out[...] = coefficients
    weights = dot_tn(lower_inverse, coefficients, HIGHEST)
    weight_high = weights.astype(BF16)
    weight_rest = (weights - weight_high.astype(F32)).astype(BF16)
    removed = dot_nn(panel_ref[...], weight_high) + dot_nn(panel_ref[...], weight_rest)
    source = jnp.where(block == 0, first_ref[...], jnp.where(block == 1, second_ref[...], third_ref[...]))
    proj_out[...] = (source.astype(F32) - removed).astype(BF16)


def shards(n_row, n_col, sparse_tiles, tile_columns, block_counts, krylov_first, panel_block):
    row_blocks, degree, tile, _ = sparse_tiles.shape
    rows_dev, width = panel_block.shape
    strip = width // n_row
    n_chip = n_row // 2
    vmem = pl.BlockSpec(memory_space=pltpu.VMEM)
    smem = pl.BlockSpec(memory_space=pltpu.SMEM)
    dma = pltpu.SemaphoreType.DMA
    shape = jax.ShapeDtypeStruct
    call = pl.pallas_call(
        functools.partial(body, n_row, n_col, degree, row_blocks, tile),
        out_shape=[
            shape((width, width), F32),
            shape((width, width), F32),
            shape((width, 3 * width), F32),
            shape((rows_dev, width), BF16),
            shape((rows_dev, width), BF16),
        ],
        in_specs=[pl.BlockSpec(memory_space=pl.ANY), smem, smem, vmem, vmem],
        out_specs=[vmem] * 5,
        scratch_shapes=[
            pltpu.VMEM(sparse_tiles.shape, BF16),
            pltpu.VMEM((row_blocks * tile, n_row * rows_dev), BF16),
            pltpu.VMEM((n_row, rows_dev, width), BF16),
            pltpu.VMEM((n_row, rows_dev, width), BF16),
            pltpu.VMEM((n_col, rows_dev, width), BF16),
            pltpu.VMEM((row_blocks * tile, width), F32),
            *[pltpu.VMEM((n_col, rows_dev, width), BF16)] * 4,
            pltpu.VMEM((4, 2, n_chip, strip, width), F32),
            *[pltpu.VMEM((4, n_chip, strip, width), F32)] * 3,
            pltpu.VMEM((4, n_col, strip, width), F32),
            pltpu.VMEM((4, 2, n_chip, strip, width), F32),
            pltpu.VMEM((width, n_col * rows_dev), BF16),
            dma,
            *[dma((2, n_chip))] * 4,
            *[dma((n_col,))] * 2,
            *[dma((2, n_col))] * 2,
            *[dma((4,))] * 2,
            *[dma((4, n_chip))] * 2,
            *[dma((4, n_col))] * 2,
            *[dma((4, n_chip))] * 4,
        ],
        compiler_params=pltpu.CompilerParams(collective_id=0, has_side_effects=True),
        name="range_finder",
    )
    lower, upper, cross, second, third = call(
        sparse_tiles, tile_columns, block_counts.reshape(1, row_blocks), krylov_first, panel_block
    )
    return tuple(pl.pallas_call(
        project,
        out_shape=[
            shape((width, width), F32),
            shape((width, 3 * width), F32),
            shape((rows_dev, 3 * width), BF16),
        ],
        grid=(3,),
        in_specs=[
            pl.BlockSpec((width, width), lambda j: (0, 0)),
            pl.BlockSpec((width, width), lambda j: (0, 0)),
            pl.BlockSpec((width, width), lambda j: (0, j)),
            *[pl.BlockSpec((rows_dev, width), lambda j: (0, 0))] * 4,
        ],
        out_specs=[
            pl.BlockSpec((width, width), lambda j: (0, 0)),
            pl.BlockSpec((width, width), lambda j: (0, j)),
            pl.BlockSpec((rows_dev, width), lambda j: (0, j)),
        ],
        name="project",
    )(lower, upper, cross, krylov_first, second, third, panel_block))


def solution(mesh):
    n_row, n_col = mesh.shape["row"], mesh.shape["col"]
    in_specs = (
        P(("row", "col"), None, None, None),
        P(("row", "col"), None),
        P(("row", "col")),
        P(("row", "col"), None),
        P(("row", "col"), None),
    )
    out_specs = (P(), P(), P(("row", "col"), None))
    return jax.shard_map(
        functools.partial(shards, n_row, n_col), mesh=mesh, in_specs=in_specs, out_specs=out_specs, check_vma=False
    )
```

```python
import functools

import jax
import jax.numpy as jnp
from jax import lax
from jax.experimental import pallas as pl
from jax.experimental.pallas import tpu as pltpu
from jax.sharding import PartitionSpec as P

HIGHEST = lax.Precision.HIGHEST
F32 = jnp.float32
BF16 = jnp.bfloat16


def dot_nn(a, b, precision=None):
    return lax.dot_general(a, b, (((1,), (0,)), ((), ())), precision=precision, preferred_element_type=F32)


def dot_nt(a, b, precision=None):
    return lax.dot_general(a, b, (((1,), (1,)), ((), ())), precision=precision, preferred_element_type=F32)


def dot_tn(a, b, precision=None):
    return lax.dot_general(a, b, (((0,), (0,)), ((), ())), precision=precision, preferred_element_type=F32)


def eliminate(diag):
    width = diag.shape[0]
    wide = (8, 2 * width)
    low = lax.broadcasted_iota(jnp.int32, (width, width), 0)
    high = lax.broadcasted_iota(jnp.int32, (width, width), 1)
    sub = lax.broadcasted_iota(jnp.int32, wide, 0)
    work = jnp.concatenate([diag, (low == high).astype(F32)], axis=1)
    head = [jnp.broadcast_to(work[:8, k : k + 1], wide) for k in range(8)]
    done = []
    for at in range(0, width, 8):
        rest = width - at - 8
        rows, below = work[:8], work[8:]
        if rest:
            tail = [jnp.broadcast_to(below[:, at + k : at + k + 1], (rest, 2 * width)) for k in range(8)]
            ahead = [jnp.broadcast_to(below[:8, at + k + 8 : at + k + 9], wide) for k in range(8)]
        scale = jnp.zeros(wide, F32)
        for i in range(8):
            inverse = 1.0 / jnp.broadcast_to(head[i][i : i + 1], wide)
            factor = jnp.where(sub > i, head[i] * inverse, 0.0)
            scale = jnp.where(sub == i, inverse, scale)
            if rest:
                under = tail[i] * inverse[:1]
                for k in range(8):
                    ahead[k] = ahead[k] - under[:8] * tail[i][k : k + 1]
                for k in range(i + 1, 8):
                    tail[k] = tail[k] - under * head[k][i : i + 1]
                below = below - under * rows[i : i + 1]
            for k in range(i + 1, 8):
                head[k] = head[k] - factor * head[k][i : i + 1]
            rows = rows - factor * rows[i : i + 1]
        done.append(rows * jnp.sqrt(scale))
        if rest:
            head, work = ahead, below
        yield None
    both = jnp.concatenate(done, axis=0)
    upper = jnp.where(high >= low, both[:, :width], 0.0)
    inverse = jnp.where(high <= low, both[:, width:], 0.0)
    yield upper, inverse


def body(n_row, n_col, degree, row_blocks, tile,
         tiles_hbm, columns_hbm, counts_hbm, first_hbm, panel_hbm,
         upper_out, coef_out, proj_out,
         tiles_ref, columns_ref, counts_ref, first_ref, panel_ref, second_ref,
         dense_ref, gathered_a, gathered_b, panels_ref, own_ref, send_a, send_b, get_a, get_b, turned_ref,
         g_refs, p_refs, q_refs, w_refs, lower_ref,
         load_sem, gather_1_sems, gather_2_sems, panel_sems, scatter_1_sems, scatter_2_sems,
         g_sems, p_sems, q_sems, w_sems):
    row = lax.axis_index("row")
    col = lax.axis_index("col")
    width = panel_ref.shape[1]
    rows_dev = panel_ref.shape[0]
    n_chip = n_row // 2
    chip = row // 2
    core = lax.rem(row, 2)
    other = 1 - core
    partner = chip * 2 + other
    mesh_type = pl.DeviceIdType.MESH

    def ahead(step):
        return lax.rem(chip + step, n_chip)

    def behind(step):
        return lax.rem(chip + n_chip - step, n_chip)

    def col_peer(step):
        return lax.rem(col + step, n_col)

    barrier = pltpu.get_barrier_semaphore()
    for step in range(1, n_col):
        pl.semaphore_signal(barrier, inc=1, device_id=(row, col_peer(step)), device_id_type=mesh_type)
    for step in range(1, n_chip):
        pl.semaphore_signal(barrier, inc=1, device_id=(ahead(step) * 2 + core, col), device_id_type=mesh_type)
    pl.semaphore_signal(barrier, inc=1, device_id=(partner, col), device_id_type=mesh_type)

    loads = [
        pltpu.make_async_copy(source, target, load_sem.at[index])
        for index, (source, target) in enumerate((
            (panel_hbm, panel_ref), (first_hbm, first_ref), (columns_hbm, columns_ref),
            (counts_hbm, counts_ref), (tiles_hbm, tiles_ref)))
    ]
    for load in loads:
        load.start()

    everything = []

    def begin(copies):
        for copy in copies:
            copy.start()
        everything.extend(copies)
        return copies

    def arrive(copies):
        for copy in copies:
            copy.wait_recv()

    def to_partner(source, target, send_sem, recv_sem):
        return pltpu.make_async_remote_copy(
            src_ref=source, dst_ref=target, send_sem=send_sem, recv_sem=recv_sem,
            device_id=(partner, col), device_id_type=mesh_type)

    def over_chips(source, target, sems):
        return [
            pltpu.make_async_remote_copy(
                src_ref=source(step), dst_ref=target(step),
                send_sem=sems.at[0, step], recv_sem=sems.at[1, step],
                device_id=(ahead(step) * 2 + core, col), device_id_type=mesh_type)
            for step in range(1, n_chip)
        ]

    def to_col(step, source, target, sems):
        return pltpu.make_async_remote_copy(
            src_ref=source, dst_ref=target, send_sem=sems.at[0, step], recv_sem=sems.at[1, step],
            device_id=(row, col_peer(step)), device_id_type=mesh_type)

    def gather(source, slots, sems):
        far, near = sems
        copies = begin(over_chips(lambda s: source, lambda s: slots(core, chip), far))
        passed = begin([to_partner(source, slots(core, chip), near.at[0, 0], near.at[1, 0])])
        return copies, passed

    def relay(state, slots, sems):
        copies, passed = state
        far, near = sems
        passed = list(passed)
        for step, copy in enumerate(copies, start=1):
            copy.wait_recv()
            here = slots(core, behind(step))
            passed += begin([to_partner(here, here, near.at[0, step], near.at[1, step])])
        return passed

    def fold(part_ref, core_ref, sems):
        return begin([to_partner(part_ref.at[other], core_ref, sems.at[0], sems.at[1])])

    def spread(folded, part_ref, core_ref, half_ref, take_ref, sems):
        arrive(folded)
        half_ref[...] = (part_ref[core].astype(F32) + core_ref[...].astype(F32)).astype(half_ref.dtype)
        return begin(over_chips(lambda s: half_ref.at[ahead(s)], lambda s: take_ref.at[s], sems))

    def strip_sum(copies, half_ref, take_ref):
        total = half_ref[chip].astype(F32)
        arrive(copies)
        for step in range(1, n_chip):
            total = total + take_ref[step].astype(F32)
        return total

    class Stage:
        def __init__(self, refs, sems):
            self.part, self.core, self.half, self.take, self.full, *self.mixes = refs
            self.fold_sems, self.spread_sems, self.far_sems, self.near_sems, *self.mix_sems = sems

        def slots(self, k, q):
            return self.full.at[k, q]

        def put(self, value, at):
            shape = self.part.shape[:3] + (value.shape[1],)
            self.part[:, :, :, at : at + value.shape[1]] = value.reshape(shape)

        def fold(self):
            self.copies = fold(self.part, self.core, self.fold_sems)

        def spread(self):
            self.copies = spread(self.copies, self.part, self.core, self.half, self.take, self.spread_sems)

        def exchange(self):
            mix, sems = self.mixes[0], self.mix_sems[0]
            mix[col] = strip_sum(self.copies, self.half, self.take).astype(mix.dtype)
            self.copies = begin([to_col(step, mix.at[col], mix.at[col], sems) for step in range(1, n_col)])

        def share(self):
            arrive(self.copies)
            mix = self.mixes[0]
            total = mix[0].astype(F32)
            for c in range(1, n_col):
                total = total + mix[c].astype(F32)
            self.publish(total)

        def gather_strips(self):
            self.publish(strip_sum(self.copies, self.half, self.take))

        def publish(self, total):
            self.full[core, chip] = total.astype(self.full.dtype)
            self.copies = gather(self.full.at[core, chip], self.slots, (self.far_sems, self.near_sems))

        def relay(self):
            self.copies = relay(self.copies, self.slots, (self.far_sems, self.near_sems))

        def whole(self):
            arrive(self.copies)
            return self.full[...].reshape(width, self.full.shape[3])

    gram_stage, pair_stage, last_stage = Stage(g_refs, g_sems), Stage(p_refs, p_sems), Stage(q_refs, q_sems)
    w_part, w_core, w_half, w_take = w_refs
    w_fold_sems, w_spread_sems = w_sems

    def product(gathered_ref, send_ref, get_ref, sems):
        right = gathered_ref[...].reshape(n_row * rows_dev, width)
        copies = []
        for step in range(1, n_col):
            peer = col_peer(step)
            block = dense_ref[pl.ds(pl.multiple_of(peer * rows_dev, rows_dev), rows_dev), :]
            send_ref[peer] = dot_nn(block, right).astype(BF16)
            copies += begin([to_col(step, send_ref.at[peer], get_ref.at[step], sems)])
        block = dense_ref[pl.ds(pl.multiple_of(col * rows_dev, rows_dev), rows_dev), :]
        own_ref[...] = dot_nn(block, right)
        return copies

    def collect(copies, get_ref):
        own = own_ref[...]
        arrive(copies)
        for step in range(1, n_col):
            own = own + get_ref[step].astype(F32)
        return own.astype(BF16)

    def slots_a(k, q):
        return gathered_a.at[q * 2 + k]

    def slots_b(k, q):
        return gathered_b.at[q * 2 + k]

    loads[0].wait()
    loads[1].wait()
    panel = panel_ref[...]
    pair_stage.put(dot_tn(panel, first_ref[...]), 0)
    pl.semaphore_wait(barrier, n_chip + n_col - 1)

    panels = begin([to_col(step, panel_ref, panels_ref.at[col], panel_sems) for step in range(1, n_col)])
    gather_1 = gather(first_ref, slots_a, gather_1_sems)
    gathered_a[row] = first_ref[...]
    panels_ref[col] = panel

    for load in loads[2:]:
        load.wait()
    column_blocks = n_row * rows_dev // tile

    def place(b):
        for j in range(column_blocks):
            slot = jnp.int32(0)
            live = jnp.int32(0)
            for k in range(degree):
                hit = jnp.logical_and(columns_ref[b, k] == j, k < counts_ref[0, b])
                slot = jnp.where(hit, k, slot)
                live = jnp.where(hit, 1, live)
            value = tiles_ref[b, slot]
            dense_ref[pl.ds(b * tile, tile), j * tile : (j + 1) * tile] = jnp.where(
                live > 0, value, jnp.zeros_like(value))

    if row_blocks <= 4:
        for b in range(row_blocks):
            place(b)
    else:
        def place_one(b, carry):
            place(b)
            return carry

        lax.fori_loop(0, row_blocks, place_one, 0)

    passed_1 = relay(gather_1, slots_a, gather_1_sems)
    arrive(panels)
    panel_rows = panels_ref[...].reshape(n_col * rows_dev, width)
    turned_ref[...] = panel_rows.T
    gram_stage.put(dot_nn(turned_ref[...], panel_rows), 0)
    gram_stage.fold()
    arrive(passed_1)
    scatter_1 = product(gathered_a, send_a, get_a, scatter_1_sems)
    for r in range(n_row):
        block = dense_ref[:, r * rows_dev : (r + 1) * rows_dev]
        w_part[r % 2, r // 2] = dot_nn(turned_ref[...], block).astype(w_part.dtype)
    w_folded = fold(w_part, w_core, w_fold_sems)
    gram_stage.spread()
    send_a[col] = own_ref[...].astype(BF16)
    pair_stage.put(dot_nn(turned_ref[...], send_a[...].reshape(n_col * rows_dev, width)), width)
    pair_stage.fold()
    w_copies = spread(w_folded, w_part, w_core, w_half, w_take, w_spread_sems)
    gram_stage.gather_strips()
    pair_stage.spread()
    gram_stage.relay()
    second_ref[...] = collect(scatter_1, get_a)
    gather_2 = gather(second_ref, slots_b, gather_2_sems)
    turned_sum = strip_sum(w_copies, w_half, w_take)
    turned_high = turned_sum.astype(BF16)
    turned_rest = (turned_sum - turned_high.astype(F32)).astype(BF16)
    last_stage.put(dot_nn(turned_high, second_ref[...]) + dot_nn(turned_rest, second_ref[...]), 0)
    last_stage.fold()
    gathered_b[row] = second_ref[...]
    pair_stage.exchange()

    pieces = 4
    size = width // pieces
    identity = (lax.broadcasted_iota(jnp.int32, (size, width), 1)
                - lax.broadcasted_iota(jnp.int32, (size, width), 0))

    def factorize():
        gram = gram_stage.whole()
        columns = [gram[size * j :, size * j : size * (j + 1)] for j in range(pieces)]
        unders = []
        for b in range(pieces):
            for pair in eliminate(columns[b][:size]):
                if pair is None:
                    yield
            upper, inverse = pair
            strips = [jnp.zeros((size, b * size), F32)] if b else []
            strips.append(upper)
            if b < pieces - 1:
                under = dot_nt(columns[b][size:], inverse, HIGHEST)
                for j in range(b + 1, pieces):
                    o = (j - b - 1) * size
                    columns[j] = columns[j] - dot_nt(under[o:], under[o : o + size], HIGHEST)
                unders.append(under)
                strips.append(under.T)
            target = (identity == b * size).astype(F32)
            for e in range(b):
                o = (b - e - 1) * size
                target = target - dot_nn(unders[e][o : o + size], lower_ref[e * size : (e + 1) * size, :], HIGHEST)
            lower_ref[b * size : (b + 1) * size, :] = dot_nn(inverse, target, HIGHEST)
            upper_out[b * size : (b + 1) * size, :] = jnp.concatenate(strips, axis=1)

    factor_steps = factorize()

    def work(count):
        for _ in range(count):
            next(factor_steps, None)

    work(4)
    last_stage.spread()
    work(7)
    passed_2 = relay(gather_2, slots_b, gather_2_sems)
    last_stage.exchange()
    arrive(passed_2)
    scatter_2 = product(gathered_b, send_b, get_b, scatter_2_sems)
    pair_stage.share()
    work(8)
    last_stage.share()
    pair_stage.relay()
    work(8)
    last_stage.relay()
    work(9)
    lower_inverse = lower_ref[...]

    def remove(cross, at):
        coefficients = dot_nn(lower_inverse, cross, HIGHEST)
        coef_out[:, at : at + cross.shape[1]] = coefficients
        weights = dot_tn(lower_inverse, coefficients, HIGHEST)
        high = weights.astype(BF16)
        rest = (weights - high.astype(F32)).astype(BF16)
        return dot_nn(panel_ref[...], high) + dot_nn(panel_ref[...], rest)

    removed = remove(pair_stage.whole().astype(F32), 0)
    proj_out[:, :width] = (first_ref[...].astype(F32) - removed[:, :width]).astype(BF16)
    proj_out[:, width : 2 * width] = (second_ref[...].astype(F32) - removed[:, width:]).astype(BF16)
    removed = remove(last_stage.whole().astype(F32), 2 * width)
    third = collect(scatter_2, get_b)
    proj_out[:, 2 * width :] = (third.astype(F32) - removed).astype(BF16)
    for copy in everything:
        copy.wait_send()


def finish(upper_ref, coef_ref, proj_ref, upper_out, coef_out, proj_out):
    upper_out[...] = upper_ref[...]
    coef_out[...] = coef_ref[...]
    proj_out[...] = proj_ref[...]


def shards(n_row, n_col, sparse_tiles, tile_columns, block_counts, krylov_first, panel_block):
    row_blocks, degree, tile, _ = sparse_tiles.shape
    rows_dev, width = panel_block.shape
    strip = width // n_row
    n_chip = n_row // 2
    vmem = pl.BlockSpec(memory_space=pltpu.VMEM)
    hbm = pl.BlockSpec(memory_space=pl.ANY)
    dma = pltpu.SemaphoreType.DMA
    shape = jax.ShapeDtypeStruct
    block = (rows_dev, width)

    def stage_refs(wide, full_type, *mix_types):
        return (
            pltpu.VMEM((2, n_chip, strip, wide), F32),
            pltpu.VMEM((n_chip, strip, wide), F32),
            pltpu.VMEM((n_chip, strip, wide), F32),
            pltpu.VMEM((n_chip, strip, wide), F32),
            pltpu.VMEM((2, n_chip, strip, wide), full_type),
            *[pltpu.VMEM((n_col, strip, wide), mix_type) for mix_type in mix_types],
        )

    def stage_sems():
        return dma((2,)), dma((2, n_chip)), dma((2, n_chip)), dma((2, n_chip))

    outs = [shape((width, width), F32), shape((width, 3 * width), F32), shape((rows_dev, 3 * width), BF16)]
    call = pl.pallas_call(
        functools.partial(body, n_row, n_col, degree, row_blocks, tile),
        out_shape=outs,
        in_specs=[hbm] * 5,
        out_specs=[vmem] * 3,
        scratch_shapes=[
            pltpu.VMEM(sparse_tiles.shape, BF16),
            pltpu.SMEM(tile_columns.shape, jnp.int32),
            pltpu.SMEM((1, row_blocks), jnp.int32),
            *[pltpu.VMEM(block, BF16)] * 3,
            pltpu.VMEM((row_blocks * tile, n_row * rows_dev), BF16),
            *[pltpu.VMEM((n_row,) + block, BF16)] * 2,
            pltpu.VMEM((n_col,) + block, BF16),
            pltpu.VMEM(block, F32),
            *[pltpu.VMEM((n_col,) + block, BF16)] * 4,
            pltpu.VMEM((width, n_col * rows_dev), BF16),
            stage_refs(width, F32),
            stage_refs(2 * width, F32, BF16),
            stage_refs(width, BF16, BF16),
            (
                pltpu.VMEM((2, n_chip, width, rows_dev), F32),
                pltpu.VMEM((n_chip, width, rows_dev), F32),
                *[pltpu.VMEM((n_chip, width, rows_dev), BF16)] * 2,
            ),
            pltpu.VMEM((width, width), F32),
            dma((5,)),
            *[(dma((2, n_chip)), dma((2, n_chip)))] * 2,
            *[dma((2, n_col))] * 3,
            stage_sems(),
            *[stage_sems() + (dma((2, n_col)),)] * 2,
            (dma((2,)), dma((2, n_chip))),
        ],
        compiler_params=pltpu.CompilerParams(collective_id=0, has_side_effects=True),
        name="range_finder",
    )
    done = call(sparse_tiles, tile_columns, block_counts.reshape(1, row_blocks), krylov_first, panel_block)
    return tuple(pl.pallas_call(
        finish,
        out_shape=outs,
        in_specs=[vmem] * 3,
        out_specs=[vmem] * 3,
        name="finish",
    )(*done))


def solution(mesh):
    n_row, n_col = mesh.shape["row"], mesh.shape["col"]
    in_specs = (
        P(("row", "col"), None, None, None),
        P(("row", "col"), None),
        P(("row", "col")),
        P(("row", "col"), None),
        P(("row", "col"), None),
    )
    out_specs = (P(), P(), P(("row", "col"), None))
    return jax.shard_map(
        functools.partial(shards, n_row, n_col), mesh=mesh, in_specs=in_specs, out_specs=out_specs, check_vma=False
    )
```

```python
import functools

import jax
import jax.numpy as jnp
from jax import lax
from jax.experimental import pallas as pl
from jax.experimental.pallas import tpu as pltpu
from jax.sharding import PartitionSpec as P

HIGHEST = lax.Precision.HIGHEST
F32 = jnp.float32
BF16 = jnp.bfloat16


def dot_nn(a, b, precision=None):
    return lax.dot_general(a, b, (((1,), (0,)), ((), ())), precision=precision, preferred_element_type=F32)


def dot_nt(a, b, precision=None):
    return lax.dot_general(a, b, (((1,), (1,)), ((), ())), precision=precision, preferred_element_type=F32)


def dot_tn(a, b, precision=None):
    return lax.dot_general(a, b, (((0,), (0,)), ((), ())), precision=precision, preferred_element_type=F32)


def eliminate(diag):
    width = diag.shape[0]
    wide = (8, 2 * width)
    low = lax.broadcasted_iota(jnp.int32, (width, width), 0)
    high = lax.broadcasted_iota(jnp.int32, (width, width), 1)
    sub = lax.broadcasted_iota(jnp.int32, wide, 0)
    work = jnp.concatenate([diag, (low == high).astype(F32)], axis=1)
    head = [jnp.broadcast_to(work[:8, k : k + 1], wide) for k in range(8)]
    done = []
    for at in range(0, width, 8):
        rest = width - at - 8
        rows, below = work[:8], work[8:]
        if rest:
            tail = [jnp.broadcast_to(below[:, at + k : at + k + 1], (rest, 2 * width)) for k in range(8)]
            ahead = [jnp.broadcast_to(below[:8, at + k + 8 : at + k + 9], wide) for k in range(8)]
        scale = jnp.zeros(wide, F32)
        for i in range(8):
            inverse = 1.0 / jnp.broadcast_to(head[i][i : i + 1], wide)
            factor = jnp.where(sub > i, head[i] * inverse, 0.0)
            scale = jnp.where(sub == i, inverse, scale)
            if rest:
                under = tail[i] * inverse[:1]
                for k in range(8):
                    ahead[k] = ahead[k] - under[:8] * tail[i][k : k + 1]
                for k in range(i + 1, 8):
                    tail[k] = tail[k] - under * head[k][i : i + 1]
                below = below - under * rows[i : i + 1]
            for k in range(i + 1, 8):
                head[k] = head[k] - factor * head[k][i : i + 1]
            rows = rows - factor * rows[i : i + 1]
        done.append(rows * jnp.sqrt(scale))
        if rest:
            head, work = ahead, below
        yield None
    both = jnp.concatenate(done, axis=0)
    upper = jnp.where(high >= low, both[:, :width], 0.0)
    inverse = jnp.where(high <= low, both[:, width:], 0.0)
    yield upper, inverse


def body(n_row, n_col, degree, row_blocks, tile,
         tiles_hbm, columns_hbm, counts_hbm, first_hbm, panel_hbm,
         upper_out, coef_out, proj_out,
         tiles_ref, columns_ref, counts_ref, first_ref, panel_ref, second_ref,
         dense_ref, gathered_a, gathered_b, panels_ref, own_ref, send_a, send_b, get_a, get_b, rest_a, turned_ref,
         sum_refs, share_refs, lower_ref,
         load_sem, gather_1_sems, gather_2_sems, panel_sems, scatter_1_sems, scatter_2_sems,
         sum_sems, share_sems):
    row = lax.axis_index("row")
    col = lax.axis_index("col")
    width = panel_ref.shape[1]
    rows_dev = panel_ref.shape[0]
    n_chip = n_row // 2
    chip = row // 2
    core = lax.rem(row, 2)
    other = 1 - core
    partner = chip * 2 + other
    mesh_type = pl.DeviceIdType.MESH

    def ahead(step):
        return lax.rem(chip + step, n_chip)

    def behind(step):
        return lax.rem(chip + n_chip - step, n_chip)

    def col_peer(step):
        return lax.rem(col + step, n_col)

    barrier = pltpu.get_barrier_semaphore()
    for step in range(1, n_col):
        pl.semaphore_signal(barrier, inc=1, device_id=(row, col_peer(step)), device_id_type=mesh_type)
    for step in range(1, n_chip):
        pl.semaphore_signal(barrier, inc=1, device_id=(ahead(step) * 2 + core, col), device_id_type=mesh_type)
    pl.semaphore_signal(barrier, inc=1, device_id=(partner, col), device_id_type=mesh_type)

    loads = [
        pltpu.make_async_copy(source, target, load_sem.at[index])
        for index, (source, target) in enumerate((
            (panel_hbm, panel_ref), (first_hbm, first_ref), (columns_hbm, columns_ref),
            (counts_hbm, counts_ref), (tiles_hbm, tiles_ref)))
    ]
    for load in loads:
        load.start()

    everything = []

    def begin(copies):
        for copy in copies:
            copy.start()
        everything.extend(copies)
        return copies

    def arrive(copies):
        for copy in copies:
            copy.wait_recv()

    def to_partner(source, target, send_sem, recv_sem):
        return pltpu.make_async_remote_copy(
            src_ref=source, dst_ref=target, send_sem=send_sem, recv_sem=recv_sem,
            device_id=(partner, col), device_id_type=mesh_type)

    def over_chips(source, target, sems):
        return [
            pltpu.make_async_remote_copy(
                src_ref=source(step), dst_ref=target(step),
                send_sem=sems.at[0, step], recv_sem=sems.at[1, step],
                device_id=(ahead(step) * 2 + core, col), device_id_type=mesh_type)
            for step in range(1, n_chip)
        ]

    def to_col(step, source, target, sems):
        return pltpu.make_async_remote_copy(
            src_ref=source, dst_ref=target, send_sem=sems.at[0, step], recv_sem=sems.at[1, step],
            device_id=(row, col_peer(step)), device_id_type=mesh_type)

    def gather(source, slots, sems):
        far, near = sems
        copies = begin(over_chips(lambda s: source, lambda s: slots(core, chip), far))
        passed = begin([to_partner(source, slots(core, chip), near.at[0, 0], near.at[1, 0])])
        return copies, passed

    def relay(state, slots, sems):
        copies, passed = state
        far, near = sems
        passed = list(passed)
        for step, copy in enumerate(copies, start=1):
            copy.wait_recv()
            here = slots(core, behind(step))
            passed += begin([to_partner(here, here, near.at[0, step], near.at[1, step])])
        return passed

    class Sum:
        def __init__(self, refs, sems):
            self.part, self.core, self.half, self.take = refs
            self.fold_sems, self.spread_sems = sems

        def put(self, value):
            self.part[...] = value.reshape(self.part.shape)

        def fold(self):
            self.copies = begin([
                to_partner(self.part.at[other], self.core, self.fold_sems.at[0], self.fold_sems.at[1])])

        def spread(self):
            arrive(self.copies)
            self.half[...] = (self.part[core].astype(F32) + self.core[...].astype(F32)).astype(self.half.dtype)
            self.copies = begin(over_chips(
                lambda s: self.half.at[ahead(s)], lambda s: self.take.at[s], self.spread_sems))

        def total(self):
            total = self.half[chip].astype(F32)
            arrive(self.copies)
            for step in range(1, n_chip):
                total = total + self.take[step].astype(F32)
            return total

    class Share:
        def __init__(self, refs, sems):
            self.full, *self.mixes = refs
            self.far_sems, self.near_sems, *self.mix_sems = sems

        def slots(self, k, q):
            return self.full.at[k, q]

        def exchange(self, *totals):
            mix, sems = self.mixes[0], self.mix_sems[0]
            for index, total in enumerate(totals):
                mix[col, :, index * width : (index + 1) * width] = total.astype(mix.dtype)
            self.copies = begin([to_col(step, mix.at[col], mix.at[col], sems) for step in range(1, n_col)])

        def share(self):
            arrive(self.copies)
            mix = self.mixes[0]
            total = mix[0].astype(F32)
            for c in range(1, n_col):
                total = total + mix[c].astype(F32)
            self.publish(total)

        def publish(self, total):
            self.full[core, chip] = total.astype(self.full.dtype)
            self.copies = gather(self.full.at[core, chip], self.slots, (self.far_sems, self.near_sems))

        def relay(self):
            self.copies = relay(self.copies, self.slots, (self.far_sems, self.near_sems))

        def whole(self):
            arrive(self.copies)
            return self.full[...].reshape(width, self.full.shape[3])

    gram_sum, first_sum, second_sum, third_sum, turned_sum = map(Sum, sum_refs, sum_sems)
    gram_share, pair_share, third_share = map(Share, share_refs, share_sems)

    def product(gathered_ref, send_ref, get_ref, sems, rest_ref=None):
        right = gathered_ref[...].reshape(n_row * rows_dev, width)
        copies = []
        for step in range(1, n_col):
            peer = col_peer(step)
            block = dense_ref[pl.ds(pl.multiple_of(peer * rows_dev, rows_dev), rows_dev), :]
            value = dot_nn(block, right)
            send_ref[peer] = value.astype(BF16)
            if rest_ref is not None:
                rest_ref[peer] = (value - send_ref[peer].astype(F32)).astype(BF16)
            copies += begin([to_col(step, send_ref.at[peer], get_ref.at[step], sems)])
        block = dense_ref[pl.ds(pl.multiple_of(col * rows_dev, rows_dev), rows_dev), :]
        own_ref[...] = dot_nn(block, right)
        return copies

    def collect(copies, get_ref):
        own = own_ref[...]
        arrive(copies)
        for step in range(1, n_col):
            own = own + get_ref[step].astype(F32)
        return own.astype(BF16)

    def slots_a(k, q):
        return gathered_a.at[q * 2 + k]

    def slots_b(k, q):
        return gathered_b.at[q * 2 + k]

    loads[0].wait()
    loads[1].wait()
    panel = panel_ref[...]
    first_sum.put(dot_tn(panel, first_ref[...]))
    pl.semaphore_wait(barrier, n_chip + n_col - 1)

    panels = begin([to_col(step, panel_ref, panels_ref.at[col], panel_sems) for step in range(1, n_col)])
    gather_1 = gather(first_ref, slots_a, gather_1_sems)
    first_sum.fold()
    gathered_a[row] = first_ref[...]
    panels_ref[col] = panel

    for load in loads[2:]:
        load.wait()
    column_blocks = n_row * rows_dev // tile

    def place(b):
        for j in range(column_blocks):
            slot = jnp.int32(0)
            live = jnp.int32(0)
            for k in range(degree):
                hit = jnp.logical_and(columns_ref[b, k] == j, k < counts_ref[0, b])
                slot = jnp.where(hit, k, slot)
                live = jnp.where(hit, 1, live)
            value = tiles_ref[b, slot]
            dense_ref[pl.ds(b * tile, tile), j * tile : (j + 1) * tile] = jnp.where(
                live > 0, value, jnp.zeros_like(value))

    if row_blocks <= 4:
        for b in range(row_blocks):
            place(b)
    else:
        def place_one(b, carry):
            place(b)
            return carry

        lax.fori_loop(0, row_blocks, place_one, 0)

    passed_1 = relay(gather_1, slots_a, gather_1_sems)
    first_sum.spread()
    arrive(panels)
    panel_rows = panels_ref[...].reshape(n_col * rows_dev, width)
    turned_ref[...] = panel_rows.T
    gram_sum.put(dot_nn(turned_ref[...], panel_rows))
    gram_sum.fold()
    arrive(passed_1)
    scatter_1 = product(gathered_a, send_a, get_a, scatter_1_sems, rest_a)
    own = own_ref[...]
    send_a[col] = own.astype(BF16)
    rest_a[col] = (own - send_a[col].astype(F32)).astype(BF16)
    second_sum.put(dot_nn(turned_ref[...], send_a[...].reshape(n_col * rows_dev, width))
                   + dot_nn(turned_ref[...], rest_a[...].reshape(n_col * rows_dev, width)))
    second_sum.fold()
    gram_sum.spread()
    for q in range(n_chip):
        block = dot_nn(turned_ref[...], dense_ref[:, q * 2 * rows_dev : (q + 1) * 2 * rows_dev])
        turned_sum.part[0, q] = block[:, :rows_dev].astype(turned_sum.part.dtype)
        turned_sum.part[1, q] = block[:, rows_dev:].astype(turned_sum.part.dtype)
    turned_sum.fold()
    second_sum.spread()
    turned_sum.spread()
    gram_share.publish(gram_sum.total())
    pair_share.exchange(first_sum.total(), second_sum.total())
    second_ref[...] = collect(scatter_1, get_a)
    gather_2 = gather(second_ref, slots_b, gather_2_sems)
    turned_own = turned_sum.total()
    turned_high = turned_own.astype(BF16)
    turned_rest = (turned_own - turned_high.astype(F32)).astype(BF16)
    third_sum.put(dot_nn(turned_high, second_ref[...]) + dot_nn(turned_rest, second_ref[...]))
    third_sum.fold()
    gathered_b[row] = second_ref[...]
    gram_share.relay()
    pieces = 4
    size = width // pieces
    identity = (lax.broadcasted_iota(jnp.int32, (size, width), 1)
                - lax.broadcasted_iota(jnp.int32, (size, width), 0))

    def factorize():
        gram = gram_share.whole()
        columns = [gram[size * j :, size * j : size * (j + 1)] for j in range(pieces)]
        unders = []
        for b in range(pieces):
            for pair in eliminate(columns[b][:size]):
                if pair is None:
                    yield
            upper, inverse = pair
            strips = [jnp.zeros((size, b * size), F32)] if b else []
            strips.append(upper)
            if b < pieces - 1:
                under = dot_nt(columns[b][size:], inverse, HIGHEST)
                for j in range(b + 1, pieces):
                    o = (j - b - 1) * size
                    columns[j] = columns[j] - dot_nt(under[o:], under[o : o + size], HIGHEST)
                unders.append(under)
                strips.append(under.T)
            target = (identity == b * size).astype(F32)
            for e in range(b):
                o = (b - e - 1) * size
                target = target - dot_nn(unders[e][o : o + size], lower_ref[e * size : (e + 1) * size, :], HIGHEST)
            lower_ref[b * size : (b + 1) * size, :] = dot_nn(inverse, target, HIGHEST)
            upper_out[b * size : (b + 1) * size, :] = jnp.concatenate(strips, axis=1)

    factor_steps = factorize()

    def work(count):
        for _ in range(count):
            next(factor_steps, None)

    third_sum.spread()
    work(10)
    pair_share.share()
    passed_2 = relay(gather_2, slots_b, gather_2_sems)
    work(2)
    third_share.exchange(third_sum.total())
    arrive(passed_2)
    scatter_2 = product(gathered_b, send_b, get_b, scatter_2_sems)
    work(8)
    third_share.share()
    pair_share.relay()
    work(8)
    third_share.relay()
    work(10)
    lower_inverse = lower_ref[...]

    def remove(cross, at):
        coefficients = dot_nn(lower_inverse, cross, HIGHEST)
        coef_out[:, at : at + cross.shape[1]] = coefficients
        weights = dot_tn(lower_inverse, coefficients, HIGHEST)
        high = weights.astype(BF16)
        rest = (weights - high.astype(F32)).astype(BF16)
        return dot_nn(panel_ref[...], high) + dot_nn(panel_ref[...], rest)

    removed = remove(pair_share.whole().astype(F32), 0)
    proj_out[:, :width] = (first_ref[...].astype(F32) - removed[:, :width]).astype(BF16)
    proj_out[:, width : 2 * width] = (second_ref[...].astype(F32) - removed[:, width:]).astype(BF16)
    removed = remove(third_share.whole().astype(F32), 2 * width)
    third = collect(scatter_2, get_b)
    proj_out[:, 2 * width :] = (third.astype(F32) - removed).astype(BF16)
    for copy in everything:
        copy.wait_send()


def finish(upper_ref, coef_ref, proj_ref, upper_out, coef_out, proj_out):
    upper_out[...] = upper_ref[...]
    coef_out[...] = coef_ref[...]
    proj_out[...] = proj_ref[...]


def shards(n_row, n_col, sparse_tiles, tile_columns, block_counts, krylov_first, panel_block):
    row_blocks, degree, tile, _ = sparse_tiles.shape
    rows_dev, width = panel_block.shape
    strip = width // n_row
    n_chip = n_row // 2
    vmem = pl.BlockSpec(memory_space=pltpu.VMEM)
    hbm = pl.BlockSpec(memory_space=pl.ANY)
    dma = pltpu.SemaphoreType.DMA
    shape = jax.ShapeDtypeStruct
    block = (rows_dev, width)

    def sum_refs(part, half_type, part_type=F32):
        return (
            pltpu.VMEM((2, n_chip) + part, part_type),
            pltpu.VMEM((n_chip,) + part, part_type),
            pltpu.VMEM((n_chip,) + part, half_type),
            pltpu.VMEM((n_chip,) + part, half_type),
        )

    def share_refs(wide, full_type, *mix_types):
        return (
            pltpu.VMEM((2, n_chip, strip, wide), full_type),
            *[pltpu.VMEM((n_col, strip, wide), mix_type) for mix_type in mix_types],
        )

    near, far = dma((2, n_chip)), dma((2, n_chip))
    outs = [shape((width, width), F32), shape((width, 3 * width), F32), shape((rows_dev, 3 * width), BF16)]
    call = pl.pallas_call(
        functools.partial(body, n_row, n_col, degree, row_blocks, tile),
        out_shape=outs,
        in_specs=[hbm] * 5,
        out_specs=[vmem] * 3,
        scratch_shapes=[
            pltpu.VMEM(sparse_tiles.shape, BF16),
            pltpu.SMEM(tile_columns.shape, jnp.int32),
            pltpu.SMEM((1, row_blocks), jnp.int32),
            *[pltpu.VMEM(block, BF16)] * 3,
            pltpu.VMEM((row_blocks * tile, n_row * rows_dev), BF16),
            *[pltpu.VMEM((n_row,) + block, BF16)] * 2,
            pltpu.VMEM((n_col,) + block, BF16),
            pltpu.VMEM(block, F32),
            *[pltpu.VMEM((n_col,) + block, BF16)] * 5,
            pltpu.VMEM((width, n_col * rows_dev), BF16),
            (
                sum_refs((strip, width), F32), sum_refs((strip, width), F32), sum_refs((strip, width), F32),
                sum_refs((strip, width), BF16), sum_refs((width, rows_dev), BF16, BF16),
            ),
            (share_refs(width, F32), share_refs(2 * width, F32, BF16), share_refs(width, BF16, BF16)),
            pltpu.VMEM((width, width), F32),
            dma((5,)),
            *[(dma((2, n_chip)), dma((2, n_chip)))] * 2,
            *[dma((2, n_col))] * 3,
            ((dma((2,)), far),) * 5,
            ((far, near), *((far, near, dma((2, n_col))),) * 2),
        ],
        compiler_params=pltpu.CompilerParams(collective_id=0, has_side_effects=True),
        name="range_finder",
    )
    done = call(sparse_tiles, tile_columns, block_counts.reshape(1, row_blocks), krylov_first, panel_block)
    return tuple(pl.pallas_call(
        finish,
        out_shape=outs,
        in_specs=[vmem] * 3,
        out_specs=[vmem] * 3,
        name="finish",
    )(*done))


def solution(mesh):
    n_row, n_col = mesh.shape["row"], mesh.shape["col"]
    in_specs = (
        P(("row", "col"), None, None, None),
        P(("row", "col"), None),
        P(("row", "col")),
        P(("row", "col"), None),
        P(("row", "col"), None),
    )
    out_specs = (P(), P(), P(("row", "col"), None))
    return jax.shard_map(
        functools.partial(shards, n_row, n_col), mesh=mesh, in_specs=in_specs, out_specs=out_specs, check_vma=False
    )
```

```python
import functools

import jax
import jax.numpy as jnp
from jax import lax
from jax.experimental import pallas as pl
from jax.experimental.pallas import tpu as pltpu
from jax.sharding import PartitionSpec as P

HIGHEST = lax.Precision.HIGHEST
F32 = jnp.float32
BF16 = jnp.bfloat16


def dot_nn(a, b, precision=None):
    return lax.dot_general(a, b, (((1,), (0,)), ((), ())), precision=precision, preferred_element_type=F32)


def dot_nt(a, b, precision=None):
    return lax.dot_general(a, b, (((1,), (1,)), ((), ())), precision=precision, preferred_element_type=F32)


def dot_tn(a, b, precision=None):
    return lax.dot_general(a, b, (((0,), (0,)), ((), ())), precision=precision, preferred_element_type=F32)


def eliminate(diag):
    width = diag.shape[0]
    wide = (8, 2 * width)
    low = lax.broadcasted_iota(jnp.int32, (width, width), 0)
    high = lax.broadcasted_iota(jnp.int32, (width, width), 1)
    sub = lax.broadcasted_iota(jnp.int32, wide, 0)
    work = jnp.concatenate([diag, (low == high).astype(F32)], axis=1)
    head = [jnp.broadcast_to(work[:8, k : k + 1], wide) for k in range(8)]
    done = []
    for at in range(0, width, 8):
        rest = width - at - 8
        rows, below = work[:8], work[8:]
        if rest:
            tail = [jnp.broadcast_to(below[:, at + k : at + k + 1], (rest, 2 * width)) for k in range(8)]
            ahead = [jnp.broadcast_to(below[:8, at + k + 8 : at + k + 9], wide) for k in range(8)]
        scale = jnp.zeros(wide, F32)
        for i in range(8):
            inverse = 1.0 / jnp.broadcast_to(head[i][i : i + 1], wide)
            factor = jnp.where(sub > i, head[i] * inverse, 0.0)
            scale = jnp.where(sub == i, inverse, scale)
            if rest:
                under = tail[i] * inverse[:1]
                for k in range(8):
                    ahead[k] = ahead[k] - under[:8] * tail[i][k : k + 1]
                for k in range(i + 1, 8):
                    tail[k] = tail[k] - under * head[k][i : i + 1]
                below = below - under * rows[i : i + 1]
            for k in range(i + 1, 8):
                head[k] = head[k] - factor * head[k][i : i + 1]
            rows = rows - factor * rows[i : i + 1]
        done.append(rows * jnp.sqrt(scale))
        if rest:
            head, work = ahead, below
        yield None
    both = jnp.concatenate(done, axis=0)
    upper = jnp.where(high >= low, both[:, :width], 0.0)
    inverse = jnp.where(high <= low, both[:, width:], 0.0)
    yield upper, inverse


def body(n_row, n_col, degree, row_blocks, tile,
         tiles_hbm, columns_hbm, counts_hbm, first_hbm, panel_hbm,
         upper_hbm, coef_hbm, proj_hbm,
         tiles_ref, columns_ref, counts_ref, first_ref, panel_ref, second_ref,
         dense_ref, gathered_a, gathered_b, panels_ref, own_ref, send_a, send_b, get_a, get_b, rest_a, turned_ref,
         sum_refs, share_refs, lower_ref, upper_out, coef_out, proj_out, out_sem,
         load_sem, gather_1_sems, gather_2_sems, panel_sems, scatter_1_sems, scatter_2_sems,
         sum_sems, share_sems):
    row = lax.axis_index("row")
    col = lax.axis_index("col")
    width = panel_ref.shape[1]
    rows_dev = panel_ref.shape[0]
    n_chip = n_row // 2
    chip = row // 2
    core = lax.rem(row, 2)
    other = 1 - core
    partner = chip * 2 + other
    mesh_type = pl.DeviceIdType.MESH

    def ahead(step):
        return lax.rem(chip + step, n_chip)

    def behind(step):
        return lax.rem(chip + n_chip - step, n_chip)

    def col_peer(step):
        return lax.rem(col + step, n_col)

    barrier = pltpu.get_barrier_semaphore()
    for step in range(1, n_col):
        pl.semaphore_signal(barrier, inc=1, device_id=(row, col_peer(step)), device_id_type=mesh_type)
    for step in range(1, n_chip):
        pl.semaphore_signal(barrier, inc=1, device_id=(ahead(step) * 2 + core, col), device_id_type=mesh_type)
    pl.semaphore_signal(barrier, inc=1, device_id=(partner, col), device_id_type=mesh_type)

    loads = [
        pltpu.make_async_copy(source, target, load_sem.at[index])
        for index, (source, target) in enumerate((
            (panel_hbm, panel_ref), (first_hbm, first_ref), (columns_hbm, columns_ref),
            (counts_hbm, counts_ref), (tiles_hbm, tiles_ref)))
    ]
    for load in loads:
        load.start()

    everything = []

    def begin(copies):
        for copy in copies:
            copy.start()
        everything.extend(copies)
        return copies

    def arrive(copies):
        for copy in copies:
            copy.wait_recv()

    def to_partner(source, target, send_sem, recv_sem):
        return pltpu.make_async_remote_copy(
            src_ref=source, dst_ref=target, send_sem=send_sem, recv_sem=recv_sem,
            device_id=(partner, col), device_id_type=mesh_type)

    def over_chips(source, target, sems):
        return [
            pltpu.make_async_remote_copy(
                src_ref=source(step), dst_ref=target(step),
                send_sem=sems.at[0, step], recv_sem=sems.at[1, step],
                device_id=(ahead(step) * 2 + core, col), device_id_type=mesh_type)
            for step in range(1, n_chip)
        ]

    def to_col(step, source, target, sems):
        return pltpu.make_async_remote_copy(
            src_ref=source, dst_ref=target, send_sem=sems.at[0, step], recv_sem=sems.at[1, step],
            device_id=(row, col_peer(step)), device_id_type=mesh_type)

    def gather(source, slots, sems):
        far, near = sems
        copies = begin(over_chips(lambda s: source, lambda s: slots(core, chip), far))
        passed = begin([to_partner(source, slots(core, chip), near.at[0, 0], near.at[1, 0])])
        return copies, passed

    def relay(state, slots, sems):
        copies, passed = state
        far, near = sems
        passed = list(passed)
        for step, copy in enumerate(copies, start=1):
            copy.wait_recv()
            here = slots(core, behind(step))
            passed += begin([to_partner(here, here, near.at[0, step], near.at[1, step])])
        return passed

    class Sum:
        def __init__(self, refs, sems):
            self.part, self.core, self.half, self.take = refs
            self.fold_sems, self.spread_sems = sems

        def put(self, value):
            self.part[...] = value.reshape(self.part.shape)

        def fold(self):
            self.copies = begin([
                to_partner(self.part.at[other], self.core, self.fold_sems.at[0], self.fold_sems.at[1])])

        def spread(self):
            arrive(self.copies)
            self.half[...] = (self.part[core].astype(F32) + self.core[...].astype(F32)).astype(self.half.dtype)
            self.copies = begin(over_chips(
                lambda s: self.half.at[ahead(s)], lambda s: self.take.at[s], self.spread_sems))

        def total(self):
            total = self.half[chip].astype(F32)
            arrive(self.copies)
            for step in range(1, n_chip):
                total = total + self.take[step].astype(F32)
            return total

    class Share:
        def __init__(self, refs, sems):
            self.full, *self.mixes = refs
            self.far_sems, self.near_sems, *self.mix_sems = sems

        def slots(self, k, q):
            return self.full.at[k, q]

        def exchange(self, *totals):
            mix, sems = self.mixes[0], self.mix_sems[0]
            for index, total in enumerate(totals):
                mix[col, :, index * width : (index + 1) * width] = total.astype(mix.dtype)
            self.copies = begin([to_col(step, mix.at[col], mix.at[col], sems) for step in range(1, n_col)])

        def share(self):
            arrive(self.copies)
            mix = self.mixes[0]
            total = mix[0].astype(F32)
            for c in range(1, n_col):
                total = total + mix[c].astype(F32)
            self.publish(total)

        def publish(self, total):
            self.full[core, chip] = total.astype(self.full.dtype)
            self.copies = gather(self.full.at[core, chip], self.slots, (self.far_sems, self.near_sems))

        def relay(self):
            self.copies = relay(self.copies, self.slots, (self.far_sems, self.near_sems))

        def whole(self):
            arrive(self.copies)
            return self.full[...].reshape(width, self.full.shape[3])

    gram_sum, first_sum, second_sum, third_sum, turned_sum = map(Sum, sum_refs, sum_sems)
    gram_share, pair_share, third_share = map(Share, share_refs, share_sems)

    def product(gathered_ref, send_ref, get_ref, sems, rest_ref=None):
        right = gathered_ref[...].reshape(n_row * rows_dev, width)
        copies = []
        for step in range(1, n_col):
            peer = col_peer(step)
            block = dense_ref[pl.ds(pl.multiple_of(peer * rows_dev, rows_dev), rows_dev), :]
            value = dot_nn(block, right)
            send_ref[peer] = value.astype(BF16)
            if rest_ref is not None:
                rest_ref[peer] = (value - send_ref[peer].astype(F32)).astype(BF16)
            copies += begin([to_col(step, send_ref.at[peer], get_ref.at[step], sems)])
        block = dense_ref[pl.ds(pl.multiple_of(col * rows_dev, rows_dev), rows_dev), :]
        own_ref[...] = dot_nn(block, right)
        return copies

    def collect(copies, get_ref):
        own = own_ref[...]
        arrive(copies)
        for step in range(1, n_col):
            own = own + get_ref[step].astype(F32)
        return own.astype(BF16)

    def slots_a(k, q):
        return gathered_a.at[q * 2 + k]

    def slots_b(k, q):
        return gathered_b.at[q * 2 + k]

    loads[0].wait()
    loads[1].wait()
    panel = panel_ref[...]
    first_sum.put(dot_tn(panel, first_ref[...]))
    pl.semaphore_wait(barrier, n_chip + n_col - 1)

    panels = begin([to_col(step, panel_ref, panels_ref.at[col], panel_sems) for step in range(1, n_col)])
    gather_1 = gather(first_ref, slots_a, gather_1_sems)
    first_sum.fold()
    gathered_a[row] = first_ref[...]
    panels_ref[col] = panel

    for load in loads[2:]:
        load.wait()
    column_blocks = n_row * rows_dev // tile

    def place(b):
        for j in range(column_blocks):
            slot = jnp.int32(0)
            live = jnp.int32(0)
            for k in range(degree):
                hit = jnp.logical_and(columns_ref[b, k] == j, k < counts_ref[0, b])
                slot = jnp.where(hit, k, slot)
                live = jnp.where(hit, 1, live)
            value = tiles_ref[b, slot]
            dense_ref[pl.ds(b * tile, tile), j * tile : (j + 1) * tile] = jnp.where(
                live > 0, value, jnp.zeros_like(value))

    if row_blocks <= 4:
        for b in range(row_blocks):
            place(b)
    else:
        def place_one(b, carry):
            place(b)
            return carry

        lax.fori_loop(0, row_blocks, place_one, 0)

    passed_1 = relay(gather_1, slots_a, gather_1_sems)
    first_sum.spread()
    arrive(panels)
    panel_rows = panels_ref[...].reshape(n_col * rows_dev, width)
    turned_ref[...] = panel_rows.T
    gram_sum.put(dot_nn(turned_ref[...], panel_rows))
    gram_sum.fold()
    arrive(passed_1)
    scatter_1 = product(gathered_a, send_a, get_a, scatter_1_sems, rest_a)
    own = own_ref[...]
    send_a[col] = own.astype(BF16)
    rest_a[col] = (own - send_a[col].astype(F32)).astype(BF16)
    second_sum.put(dot_nn(turned_ref[...], send_a[...].reshape(n_col * rows_dev, width))
                   + dot_nn(turned_ref[...], rest_a[...].reshape(n_col * rows_dev, width)))
    second_sum.fold()
    gram_sum.spread()
    for q in range(n_chip):
        block = dot_nn(turned_ref[...], dense_ref[:, q * 2 * rows_dev : (q + 1) * 2 * rows_dev])
        turned_sum.part[0, q] = block[:, :rows_dev].astype(turned_sum.part.dtype)
        turned_sum.part[1, q] = block[:, rows_dev:].astype(turned_sum.part.dtype)
    turned_sum.fold()
    second_sum.spread()
    turned_sum.spread()
    gram_share.publish(gram_sum.total())
    pair_share.exchange(first_sum.total(), second_sum.total())
    second_ref[...] = collect(scatter_1, get_a)
    gather_2 = gather(second_ref, slots_b, gather_2_sems)
    turned_own = turned_sum.total()
    turned_high = turned_own.astype(BF16)
    turned_rest = (turned_own - turned_high.astype(F32)).astype(BF16)
    third_sum.put(dot_nn(turned_high, second_ref[...]) + dot_nn(turned_rest, second_ref[...]))
    third_sum.fold()
    gathered_b[row] = second_ref[...]
    gram_share.relay()
    pieces = 4
    size = width // pieces
    identity = (lax.broadcasted_iota(jnp.int32, (size, width), 1)
                - lax.broadcasted_iota(jnp.int32, (size, width), 0))

    def factorize():
        gram = gram_share.whole()
        columns = [gram[size * j :, size * j : size * (j + 1)] for j in range(pieces)]
        unders = []
        for b in range(pieces):
            for pair in eliminate(columns[b][:size]):
                if pair is None:
                    yield
            upper, inverse = pair
            strips = [jnp.zeros((size, b * size), F32)] if b else []
            strips.append(upper)
            if b < pieces - 1:
                under = dot_nt(columns[b][size:], inverse, HIGHEST)
                for j in range(b + 1, pieces):
                    o = (j - b - 1) * size
                    columns[j] = columns[j] - dot_nt(under[o:], under[o : o + size], HIGHEST)
                unders.append(under)
                strips.append(under.T)
            target = (identity == b * size).astype(F32)
            for e in range(b):
                o = (b - e - 1) * size
                target = target - dot_nn(unders[e][o : o + size], lower_ref[e * size : (e + 1) * size, :], HIGHEST)
            lower_ref[b * size : (b + 1) * size, :] = dot_nn(inverse, target, HIGHEST)
            upper_out[b * size : (b + 1) * size, :] = jnp.concatenate(strips, axis=1)

    factor_steps = factorize()

    def work(count):
        for _ in range(count):
            next(factor_steps, None)

    third_sum.spread()
    work(12)
    pair_share.share()
    passed_2 = relay(gather_2, slots_b, gather_2_sems)
    third_share.exchange(third_sum.total())
    arrive(passed_2)
    scatter_2 = product(gathered_b, send_b, get_b, scatter_2_sems)
    work(8)
    third_share.share()
    pair_share.relay()
    work(8)
    third_share.relay()
    work(10)
    stores = []

    def store(source, target):
        copy = pltpu.make_async_copy(source, target, out_sem.at[len(stores)])
        copy.start()
        stores.append(copy)

    store(upper_out, upper_hbm)
    lower_inverse = lower_ref[...]

    def remove(cross, at):
        coefficients = dot_nn(lower_inverse, cross, HIGHEST)
        coef_out[:, at : at + cross.shape[1]] = coefficients
        weights = dot_tn(lower_inverse, coefficients, HIGHEST)
        high = weights.astype(BF16)
        rest = (weights - high.astype(F32)).astype(BF16)
        span = slice(at, at + cross.shape[1])
        store(coef_out.at[:, span], coef_hbm.at[:, span])
        return dot_nn(panel_ref[...], high) + dot_nn(panel_ref[...], rest)

    removed = remove(pair_share.whole().astype(F32), 0)
    proj_out[:, :width] = (first_ref[...].astype(F32) - removed[:, :width]).astype(BF16)
    proj_out[:, width : 2 * width] = (second_ref[...].astype(F32) - removed[:, width:]).astype(BF16)
    store(proj_out.at[:, : 2 * width], proj_hbm.at[:, : 2 * width])
    removed = remove(third_share.whole().astype(F32), 2 * width)
    third = collect(scatter_2, get_b)
    proj_out[:, 2 * width :] = (third.astype(F32) - removed).astype(BF16)
    store(proj_out.at[:, 2 * width :], proj_hbm.at[:, 2 * width :])
    for copy in everything:
        copy.wait_send()
    for copy in stores:
        copy.wait()


def finish(upper_ref, coef_ref, proj_ref, upper_out, coef_out, proj_out):
    upper_out[...] = upper_ref[...]
    coef_out[...] = coef_ref[...]
    proj_out[...] = proj_ref[...]


def shards(n_row, n_col, sparse_tiles, tile_columns, block_counts, krylov_first, panel_block):
    row_blocks, degree, tile, _ = sparse_tiles.shape
    rows_dev, width = panel_block.shape
    strip = width // n_row
    n_chip = n_row // 2
    vmem = pl.BlockSpec(memory_space=pltpu.VMEM)
    hbm = pl.BlockSpec(memory_space=pl.ANY)
    dma = pltpu.SemaphoreType.DMA
    shape = jax.ShapeDtypeStruct
    block = (rows_dev, width)

    def sum_refs(part, half_type, part_type=F32):
        return (
            pltpu.VMEM((2, n_chip) + part, part_type),
            pltpu.VMEM((n_chip,) + part, part_type),
            pltpu.VMEM((n_chip,) + part, half_type),
            pltpu.VMEM((n_chip,) + part, half_type),
        )

    def share_refs(wide, full_type, *mix_types):
        return (
            pltpu.VMEM((2, n_chip, strip, wide), full_type),
            *[pltpu.VMEM((n_col, strip, wide), mix_type) for mix_type in mix_types],
        )

    near, far = dma((2, n_chip)), dma((2, n_chip))
    outs = [shape((width, width), F32), shape((width, 3 * width), F32), shape((rows_dev, 3 * width), BF16)]
    call = pl.pallas_call(
        functools.partial(body, n_row, n_col, degree, row_blocks, tile),
        out_shape=outs,
        in_specs=[hbm] * 5,
        out_specs=[hbm] * 3,
        scratch_shapes=[
            pltpu.VMEM(sparse_tiles.shape, BF16),
            pltpu.SMEM(tile_columns.shape, jnp.int32),
            pltpu.SMEM((1, row_blocks), jnp.int32),
            *[pltpu.VMEM(block, BF16)] * 3,
            pltpu.VMEM((row_blocks * tile, n_row * rows_dev), BF16),
            *[pltpu.VMEM((n_row,) + block, BF16)] * 2,
            pltpu.VMEM((n_col,) + block, BF16),
            pltpu.VMEM(block, F32),
            *[pltpu.VMEM((n_col,) + block, BF16)] * 5,
            pltpu.VMEM((width, n_col * rows_dev), BF16),
            (
                sum_refs((strip, width), F32), sum_refs((strip, width), F32), sum_refs((strip, width), F32),
                sum_refs((strip, width), BF16), sum_refs((width, rows_dev), BF16, BF16),
            ),
            (share_refs(width, F32), share_refs(2 * width, F32, BF16), share_refs(width, BF16, BF16)),
            pltpu.VMEM((width, width), F32),
            *[pltpu.VMEM(out.shape, out.dtype) for out in outs],
            dma((5,)),
            dma((5,)),
            *[(dma((2, n_chip)), dma((2, n_chip)))] * 2,
            *[dma((2, n_col))] * 3,
            ((dma((2,)), far),) * 5,
            ((far, near), *((far, near, dma((2, n_col))),) * 2),
        ],
        compiler_params=pltpu.CompilerParams(collective_id=0, has_side_effects=True),
        name="range_finder",
    )
    done = call(sparse_tiles, tile_columns, block_counts.reshape(1, row_blocks), krylov_first, panel_block)
    return tuple(pl.pallas_call(
        finish,
        out_shape=outs,
        in_specs=[vmem] * 3,
        out_specs=[vmem] * 3,
        name="finish",
    )(*done))


def solution(mesh):
    n_row, n_col = mesh.shape["row"], mesh.shape["col"]
    in_specs = (
        P(("row", "col"), None, None, None),
        P(("row", "col"), None),
        P(("row", "col")),
        P(("row", "col"), None),
        P(("row", "col"), None),
    )
    out_specs = (P(), P(), P(("row", "col"), None))
    return jax.shard_map(
        functools.partial(shards, n_row, n_col), mesh=mesh, in_specs=in_specs, out_specs=out_specs, check_vma=False
    )
```
